32 devices in a mesh: wa: 4 (over z), ha: 8 (over y, x, core).
Axes of the slice: x: 2, y: 2, z: 4, core: 2. Of those that a mesh axis runs over, the one named last changes fastest.
Arguments:
- tokens: bfloat16 [1024, 16384], P('ha', 'wa'), may hold values from -6 to 6
- gain_attn: bfloat16 [16384], P('wa'), may hold values from 0.25 to 1.75
- w_query: bfloat16 [16384, 16384], P('wa', 'ha'), may hold values from -0.046875 to 0.046875, as said below
- w_key: bfloat16 [16384, 1024], P('wa'), may hold values from -1.171875 to 1.171875, as said below
- w_value: bfloat16 [16384, 1024], P('wa'), may hold values from -0.046875 to 0.046875
- w_out: bfloat16 [16384, 16384], P('ha', 'wa'), may hold values from -0.1875 to 0.1875
- gain_ffn: bfloat16 [16384], P('wa'), may hold values from 0.25 to 1.75
- segment_ids: int32 [1024], replicated, may hold values from 0 to 31, never falling along the last dimension, each value on 1 to 256 neighbouring positions
Outputs:
- residual_out: bfloat16 [1024, 16384], P('ha', 'wa')
- ffn_input: bfloat16 [1024, 16384], P('ha', 'wa')
The draws below stay inside these ranges and needn't reach their ends.
Inputs may be any that keep to these rules, and one draw needn't show every extreme that they name: `w_query`: entries scaled by 16384 ** -0.5. `w_key`: entries scaled by 16384 ** -0.5. `segment_ids`: segment ids never fall along the tokens; each prompt has 1 to 256 tokens and one has exactly 256.
All inputs are finite; a program needn't handle non-finite values.
Results may differ from the reference program's by a relative error of at most 0.00675.
The reference program's roundings to bfloat16 on the way (of `scaled`, `queries`, `keys`, `weights` and `head_out`) count: a program that leaves them out, or rounds other values in their place, can miss the bound.
Values may be sent and summed in bfloat16 or wider, within the bound.
A program may use at most 192 MiB of HBM per device.

```python
import math
import jax
import jax.numpy as jnp
import numpy as np
from jax import lax

D = 16384
H = 128
KVH = 8
HD = 128
TOKENS = 1024
LMAX = 256


def query_base(key):
    noise = jax.random.normal(jax.random.fold_in(key, 11), (D, H * HD), jnp.float32)
    return jnp.clip(noise, -6.0, 6.0) * D ** (-0.5)


def draw_w_query(key, part):
    return query_base(key).astype(jnp.bfloat16)


def draw_w_key(key, part):
    noise = jax.random.normal(jax.random.fold_in(key, 23), (D, KVH * HD), jnp.float32)
    noise = jnp.clip(noise, -6.0, 6.0) * D ** (-0.5)
    return noise.astype(jnp.bfloat16)


def level_of(key, extent, cuts, smallest, high):
    def one(axis_at, blocks):
        draws = jax.random.uniform(jax.random.fold_in(jax.random.fold_in(key, 6), axis_at), (blocks,), jnp.float32, smallest / len(cuts), high / len(cuts))
        return jnp.repeat(jnp.exp(draws), extent[axis_at] // blocks).reshape((-1,) + (1,) * (len(extent) - axis_at - 1))

    gain = one(*cuts[0])
    for cut in cuts[1:]:
        gain = gain * one(*cut)
    return gain


def length_profile(amount, total, bound, lean):
    weights = [(1 << 20) // math.isqrt(rank ** lean) + 1 for rank in range(2, amount + 1)]
    rest, given = total - bound - (amount - 1), [1] * (amount - 1)
    while rest > 0:
        free = [i for i in range(amount - 1) if given[i] < bound]
        pool, budget = sum([weights[i] for i in free]), rest
        for i in free:
            addition = min(bound - given[i], max(1, budget * weights[i] // pool), rest)
            given[i] = given[i] + addition
            rest = rest - addition
    return np.array([bound] + given)


def ragged_sizes(rng, amount, total, most, skew):
    if amount == 2:
        one = jax.random.randint(rng, (), max(1, total - most), min(most, total - 1) + 1)
        return jnp.stack([one, total - one])
    sizes = jnp.asarray(length_profile(amount, total, most, skew), jnp.int32)
    twos = (amount - 1) // 2
    donor, taker = sizes[1:1 + 2 * twos:2], sizes[2:2 + 2 * twos:2]
    margin = jnp.minimum(donor - 1, most - taker)
    moved = jax.random.randint(jax.random.fold_in(rng, 1), (twos,), 0, 1 << 20) % (margin + 1)
    sizes = sizes.at[1:1 + 2 * twos:2].set(donor - moved).at[2:2 + 2 * twos:2].set(taker + moved)
    return sizes[jax.random.permutation(jax.random.fold_in(rng, 2), amount)]


def gaussian(stream_key, extent, deviation, limit, cuts=(), kind=jnp.bfloat16):
    factor_of = level_of(stream_key, extent, cuts, -0.22, 0.18) if cuts else 1.0
    drawn = jax.random.normal(stream_key, extent, jnp.float32) * deviation * factor_of
    return jnp.minimum(jnp.maximum(drawn, -limit), limit).astype(kind)


def setup_inputs(seed: int = 0) -> dict:
    key_list = jax.random.split(jax.random.key(seed), 9)
    return {
        "tokens": gaussian(key_list[0], (TOKENS, D), 1.0, 6.0, ((0, 8), (1, 4))),
        "gain_attn": jnp.clip(1.0 + 0.15 * jax.random.normal(key_list[1], (D,), jnp.float32), 0.25, 1.75).astype(jnp.bfloat16),
        "w_query": draw_w_query(jax.random.fold_in(key_list[8], 71), 0),
        "w_key": draw_w_key(jax.random.fold_in(key_list[8], 71), 0),
        "w_value": gaussian(key_list[4], (D, KVH * HD), D ** -0.5, 0.046875, ((0, 4),)),
        "w_out": gaussian(key_list[5], (H * HD, D), (H * HD // 16) ** -0.5, 0.1875, ((0, 8), (1, 4))),
        "gain_ffn": jnp.clip(1.0 + 0.15 * jax.random.normal(key_list[6], (D,), jnp.float32), 0.25, 1.75).astype(jnp.bfloat16),
        "segment_ids": jnp.searchsorted(jnp.cumsum(ragged_sizes(key_list[7], TOKENS // 32, TOKENS, LMAX, 2)), jnp.arange(TOKENS), side="right").astype(jnp.int32),
    }


EPS = 1e-05

def positions(segment_ids):
    index = jnp.arange(segment_ids.shape[0], dtype=jnp.int32)
    fresh = jnp.concatenate([jnp.ones((1,), dtype=bool), segment_ids[1:] != segment_ids[:-1]])
    start = lax.cummax(jnp.where(fresh, index, jnp.zeros_like(index)), axis=0)
    return (index - start).astype(jnp.float32)

def rope_tables(position):
    half = HD // 2
    inverse = 500000.0 ** (-(jnp.arange(half, dtype=jnp.float32) * 2.0 / HD))
    angle = position[:, None] * inverse[None, :]
    return (jnp.cos(angle), jnp.sin(angle))

def rotate(values, cosine, sine):
    half = values.shape[-1] // 2
    first = values[..., :half]
    second = values[..., half:]
    cosine = cosine[:, None, :]
    sine = sine[:, None, :]
    return jnp.concatenate([first * cosine - second * sine, second * cosine + first * sine], axis=-1)

def reference(tokens, gain_attn, w_query, w_key, w_value, w_out, gain_ffn, segment_ids):
    count = tokens.shape[0]
    token_f = tokens.astype(jnp.float32)
    row_scale = lax.rsqrt(lax.optimization_barrier(jnp.mean(token_f * token_f, axis=1)) + EPS)
    scaled = (token_f * gain_attn.astype(jnp.float32)).astype(jnp.bfloat16)
    cosine, sine = rope_tables(positions(segment_ids))
    query_f = jnp.dot(scaled, w_query, preferred_element_type=jnp.float32) * row_scale[:, None]
    queries = rotate(query_f.reshape(count, H, HD), cosine, sine).astype(jnp.bfloat16)
    key_plain = (jnp.dot(scaled, w_key, preferred_element_type=jnp.float32) * row_scale[:, None]).astype(jnp.bfloat16)
    key_plain = lax.optimization_barrier(key_plain)
    keys = rotate(key_plain.astype(jnp.float32).reshape(count, KVH, HD), cosine, sine).astype(jnp.bfloat16)
    values = (jnp.dot(scaled, w_value, preferred_element_type=jnp.float32) * row_scale[:, None]).astype(jnp.bfloat16)
    values = values.reshape(count, KVH, HD)
    index = jnp.arange(count, dtype=jnp.int32)
    allowed = (segment_ids[:, None] == segment_ids[None, :]) & (index[None, :] <= index[:, None])
    grouped = queries.reshape(count, KVH, H // KVH, HD).transpose(1, 0, 2, 3)

    def one_group(items):
        query_h, key_h, value_h = items
        scores = jnp.einsum('tgd,sd->gts', query_h.astype(jnp.float32), key_h.astype(jnp.float32)) * HD ** (-0.5)
        scores = jnp.where(allowed[None], scores, -1e+30)
        peak = lax.optimization_barrier(jnp.max(scores, axis=-1, keepdims=True))
        expo = jnp.where(allowed[None], jnp.exp(scores - peak), 0.0)
        weights = (expo / lax.optimization_barrier(jnp.sum(expo, axis=-1, keepdims=True))).astype(jnp.bfloat16)
        return jnp.einsum('gts,sd->tgd', weights.astype(jnp.float32), value_h.astype(jnp.float32)).astype(jnp.bfloat16)
    head_out = lax.map(one_group, (grouped, keys.transpose(1, 0, 2), values.transpose(1, 0, 2)))
    head_out = head_out.transpose(1, 0, 2, 3).reshape(count, H * HD)
    attended = jnp.dot(head_out, w_out, preferred_element_type=jnp.float32)
    residual_out = (token_f + attended).astype(jnp.bfloat16)
    residual_f = residual_out.astype(jnp.float32)
    scale_two = lax.rsqrt(lax.optimization_barrier(jnp.mean(residual_f * residual_f, axis=1)) + EPS)
    ffn_input = (residual_f * scale_two[:, None] * gain_ffn.astype(jnp.float32)).astype(jnp.bfloat16)
    return (residual_out, ffn_input)
```

```python
import jax
import jax.numpy as jnp
from jax import lax
from jax.sharding import PartitionSpec as P

KVH = 8
HD = 128
WINDOW = 256


EPS = 1e-05


def rope_tables(position):
    half = HD // 2
    inverse = 500000.0 ** (-(jnp.arange(half, dtype=jnp.float32) * 2.0 / HD))
    angle = position[:, None] * inverse[None, :]
    return (jnp.cos(angle), jnp.sin(angle))


def rotate(values, cosine, sine):
    half = values.shape[-1] // 2
    first = values[..., :half]
    second = values[..., half:]
    cosine = cosine[:, None, :]
    sine = sine[:, None, :]
    return jnp.concatenate(
        [first * cosine - second * sine, second * cosine + first * sine], axis=-1
    )


def attend(queries, key_head, value_head, segment_ids, first):
    q_rows = queries.shape[0]
    size = min(WINDOW, q_rows)
    keys_pad = jnp.pad(key_head, ((WINDOW, 0), (0, 0)))
    values_pad = jnp.pad(value_head, ((WINDOW, 0), (0, 0)))
    segment_pad = jnp.pad(segment_ids, (WINDOW, 0), constant_values=-1)
    outs = []
    for at in range(0, q_rows, size):
        start = first + at
        query = queries[at : at + size]
        key = lax.dynamic_slice_in_dim(keys_pad, start, size + WINDOW, 0)
        value = lax.dynamic_slice_in_dim(values_pad, start, size + WINDOW, 0)
        k_segment = lax.dynamic_slice_in_dim(segment_pad, start, size + WINDOW, 0)
        q_segment = lax.dynamic_slice_in_dim(segment_ids, start, size, 0)
        k_at = jnp.arange(size + WINDOW, dtype=jnp.int32) - WINDOW
        q_at = jnp.arange(size, dtype=jnp.int32)
        allowed = (q_segment[:, None] == k_segment[None, :]) & (k_at[None, :] <= q_at[:, None])
        allowed = allowed & (k_at + start >= 0)[None, :]
        scores = jnp.einsum(
            "thd,sd->hts", query, key, preferred_element_type=jnp.float32
        ) * HD ** (-0.5)
        scores = jnp.where(allowed[None], scores, -1e30)
        peak = jnp.max(scores, axis=-1, keepdims=True)
        expo = jnp.where(allowed[None], jnp.exp(scores - peak), 0.0)
        weights = (expo / jnp.sum(expo, axis=-1, keepdims=True)).astype(jnp.bfloat16)
        out = jnp.einsum("hts,sd->thd", weights, value, preferred_element_type=jnp.float32)
        outs.append(out.astype(jnp.bfloat16))
    return jnp.concatenate(outs, axis=0)


def on_device(tokens, gain_attn, w_query, w_key, w_value, w_out, gain_ffn, segment_ids):
    rows_dev, width_dev = tokens.shape
    n_wa = lax.axis_size("wa")
    n_ha = lax.axis_size("ha")
    total = rows_dev * n_ha
    width = width_dev * n_wa
    head_cols = w_query.shape[1]
    heads_dev = head_cols // HD
    token_f = tokens.astype(jnp.float32)
    gain_one = gain_attn.astype(jnp.float32)
    kv_head = lax.axis_index("ha") // (n_ha // KVH)
    kv_weights = jnp.concatenate(
        [
            lax.dynamic_slice_in_dim(w_key, kv_head * HD, HD, 1),
            lax.dynamic_slice_in_dim(w_value, kv_head * HD, HD, 1),
        ],
        axis=1,
    )
    gathered = lax.all_gather(tokens, "ha", axis=0, tiled=True)
    gathered_f = gathered.astype(jnp.float32)
    row_sq = jnp.sum(gathered_f * gathered_f, axis=1)
    scaled = (gathered_f * gain_one).astype(jnp.bfloat16)
    kv_part = jnp.dot(scaled, kv_weights, preferred_element_type=jnp.float32)
    kv_sum = lax.psum(
        jnp.concatenate([kv_part, jnp.broadcast_to(row_sq[:, None], (total, HD))], axis=1), "wa"
    )
    row_scale = lax.rsqrt(kv_sum[:, 2 * HD] / width + EPS)
    index_all = jnp.arange(total, dtype=jnp.int32)
    fresh = jnp.concatenate([jnp.ones((1,), dtype=bool), segment_ids[1:] != segment_ids[:-1]])
    start_all = lax.cummax(jnp.where(fresh, index_all, jnp.zeros_like(index_all)), axis=0)
    cosine, sine = rope_tables((index_all - start_all).astype(jnp.float32))
    key_plain = (kv_sum[:, :HD] * row_scale[:, None]).astype(jnp.bfloat16)
    key_plain = lax.optimization_barrier(key_plain)
    value_head = (kv_sum[:, HD : 2 * HD] * row_scale[:, None]).astype(jnp.bfloat16)
    key_head = rotate(key_plain.astype(jnp.float32).reshape(total, 1, HD), cosine, sine)
    key_head = key_head.reshape(total, HD).astype(jnp.bfloat16)
    q_rows = total // n_wa
    first = lax.axis_index("wa") * q_rows
    block = scaled
    query_f = lax.psum_scatter(
        jnp.dot(block, w_query, preferred_element_type=jnp.float32),
        "wa",
        scatter_dimension=0,
        tiled=True,
    )
    q_scale = lax.dynamic_slice_in_dim(row_scale, first, q_rows, 0)
    q_cos = lax.dynamic_slice_in_dim(cosine, first, q_rows, 0)
    q_sin = lax.dynamic_slice_in_dim(sine, first, q_rows, 0)
    queries = rotate(
        (query_f * q_scale[:, None]).reshape(q_rows, heads_dev, HD), q_cos, q_sin
    ).astype(jnp.bfloat16)
    head_out = attend(queries, key_head, value_head, segment_ids, first)
    head_out = head_out.reshape(q_rows, head_cols)
    head_all = lax.all_gather(head_out, "wa", axis=0, tiled=True)
    block = head_all
    attended = lax.psum_scatter(
        jnp.dot(block, w_out, preferred_element_type=jnp.float32).astype(jnp.bfloat16),
        "ha",
        scatter_dimension=0,
        tiled=True,
    )
    residual_out = (token_f + attended.astype(jnp.float32)).astype(jnp.bfloat16)
    residual_f = residual_out.astype(jnp.float32)
    square_two = lax.psum(jnp.sum(residual_f * residual_f, axis=1), "wa")
    scale_two = lax.rsqrt(square_two / width + EPS)
    ffn_input = (residual_f * scale_two[:, None] * gain_ffn.astype(jnp.float32)).astype(
        jnp.bfloat16
    )
    return (residual_out, ffn_input)


def solution(mesh):
    in_specs = (
        P("ha", "wa"),
        P("wa"),
        P("wa", "ha"),
        P("wa", None),
        P("wa", None),
        P("ha", "wa"),
        P("wa"),
        P(),
    )
    out_specs = (P("ha", "wa"), P("ha", "wa"))
    return jax.shard_map(
        on_device, mesh=mesh, in_specs=in_specs, out_specs=out_specs, check_vma=False
    )
```

```python
import functools

import jax
import jax.numpy as jnp
from jax import lax
from jax.experimental import pallas as pl
from jax.experimental.pallas import tpu as pltpu
from jax.sharding import PartitionSpec as P

KVH = 8
HD = 128
WINDOW = 256


EPS = 1e-05


def rope_tables(position):
    half = HD // 2
    inverse = 500000.0 ** (-(jnp.arange(half, dtype=jnp.float32) * 2.0 / HD))
    angle = position[:, None] * inverse[None, :]
    return (jnp.cos(angle), jnp.sin(angle))


def rotate(values, cosine, sine):
    half = values.shape[-1] // 2
    first = values[..., :half]
    second = values[..., half:]
    cosine = cosine[:, None, :]
    sine = sine[:, None, :]
    return jnp.concatenate(
        [first * cosine - second * sine, second * cosine + first * sine], axis=-1
    )


def greet_peers(n):
    me = lax.axis_index("wa")
    barrier = pltpu.get_barrier_semaphore()
    for d in range(1, n):
        pl.semaphore_signal(
            barrier,
            inc=1,
            device_id={"wa": lax.rem(me + d, n)},
            device_id_type=pl.DeviceIdType.MESH,
        )
    pl.semaphore_wait(barrier, n - 1)


def send_to(src, dst, send_sem, recv_sem, peer):
    return pltpu.make_async_remote_copy(
        src_ref=src,
        dst_ref=dst,
        send_sem=send_sem,
        recv_sem=recv_sem,
        device_id={"wa": peer},
        device_id_type=pl.DeviceIdType.MESH,
    )


def peer_copies(n, x_ref, land, sems):
    me = lax.axis_index("wa")
    return [
        send_to(x_ref, land.at[d - 1], sems.at[0, d - 1], sems.at[1, d - 1], lax.rem(me + d, n))
        for d in range(1, n)
    ]


def peer_sum_kernel(n, x_ref, o_ref, land, sems):
    greet_peers(n)
    copies = peer_copies(n, x_ref, land, sems)
    for copy in copies:
        copy.start()
    for copy in copies:
        copy.wait()
    total = x_ref[...]
    for d in range(n - 1):
        total = total + land[d]
    o_ref[...] = total


def peer_sum(x, n):
    vmem = pl.BlockSpec(memory_space=pltpu.VMEM)
    return pl.pallas_call(
        functools.partial(peer_sum_kernel, n),
        out_shape=jax.ShapeDtypeStruct(x.shape, x.dtype),
        in_specs=[vmem],
        out_specs=vmem,
        scratch_shapes=[
            pltpu.VMEM((n - 1,) + x.shape, x.dtype),
            pltpu.SemaphoreType.DMA((2, n - 1)),
        ],
        compiler_params=pltpu.CompilerParams(
            collective_id=2, has_side_effects=True, vmem_limit_bytes=4 << 20
        ),
    )(x)


def reduce_kernel(
    n, nc, half, window, q_ref, kv_ref, sq_ref, qo, kvo, sqo,
    rq, rkv, lq, lkv, lsq, rqs, rks, lqs, lks, sqs,
):
    me = lax.axis_index("wa")
    last = n - 1
    right = jnp.minimum(me + 1, last)
    left = jnp.maximum(me - 1, 0)
    cq = half // nc
    cw = (half + window) // nc
    greet_peers(n)
    small = peer_copies(n, sq_ref, lsq, sqs)
    for copy in small:
        copy.start()
    kvo[pl.ds(0, window), :] = jnp.zeros((window, kvo.shape[1]), kvo.dtype)

    def rows(base, j, size):
        return pl.ds(pl.multiple_of(base + j * size, 8), size)

    def right_copy(j, first_hop):
        own, wide = rows(0, j, cq), rows(0, j, cw)
        if first_hop:
            src, src_kv = q_ref.at[rows(half, j, cq)], kv_ref.at[rows(half - window, j, cw)]
        else:
            src, src_kv = rq.at[own], rkv.at[wide]
        return (
            send_to(src, rq.at[own], rqs.at[0, j], rqs.at[1, j], right),
            send_to(src_kv, rkv.at[wide], rks.at[0, j], rks.at[1, j], right),
        )

    def left_copy(j, first_hop):
        own = rows(0, j, cq)
        src, src_kv = (q_ref, kv_ref) if first_hop else (lq, lkv)
        return (
            send_to(src.at[own], lq.at[own], lqs.at[0, j], lqs.at[1, j], left),
            send_to(src_kv.at[own], lkv.at[own], lks.at[0, j], lks.at[1, j], left),
        )

    @pl.loop(0, nc + last)
    def _(s):
        j = s - me
        i = s - (last - me)
        right_on = (j >= 0) & (j < nc)
        left_on = (i >= 0) & (i < nc)

        @pl.when(right_on & (me > 0))
        def _():
            for copy in right_copy(j, False):
                copy.wait_recv()
            own, wide = rows(0, j, cq), rows(0, j, cw)
            rq[own, :] = rq[own, :] + q_ref[rows(half, j, cq), :]
            rkv[wide, :] = rkv[wide, :] + kv_ref[rows(half - window, j, cw), :]

        @pl.when(left_on & (me < last))
        def _():
            for copy in left_copy(i, False):
                copy.wait_recv()
            own = rows(0, i, cq)
            lq[own, :] = lq[own, :] + q_ref[own, :]
            lkv[own, :] = lkv[own, :] + kv_ref[own, :]

        @pl.when(right_on & (me == 0))
        def _():
            for copy in right_copy(j, True):
                copy.start()

        @pl.when(left_on & (me == last))
        def _():
            for copy in left_copy(i, True):
                copy.start()

        @pl.when(right_on & (me > 0) & (me < last))
        def _():
            for copy in right_copy(j, False):
                copy.start()

        @pl.when(left_on & (me > 0) & (me < last))
        def _():
            for copy in left_copy(i, False):
                copy.start()

        @pl.when(right_on & (me == last))
        def _():
            own, wide = rows(0, j, cq), rows(0, j, cw)
            qo[own, :] = rq[own, :]
            kvo[wide, :] = rkv[wide, :]

        @pl.when(left_on & (me < last))
        def _():
            own = rows(0, i, cq)
            qo[own, :] = lq[own, :]
            kvo[rows(window, i, cq), :] = lkv[own, :]

    @pl.loop(0, nc)
    def _(j):
        @pl.when(me < last)
        def _():
            for copy in right_copy(j, False):
                copy.wait_send()

        @pl.when(me > 0)
        def _():
            for copy in left_copy(j, False):
                copy.wait_send()

    for copy in small:
        copy.wait()
    total = sq_ref[...]
    for d in range(n - 1):
        total = total + lsq[d]
    sqo[...] = total


def reduce_to_ends(q_part, kv_part, row_sq, n, window):
    rows, cols = q_part.shape
    kv_cols = kv_part.shape[1]
    half = rows // 2
    nc = half // 16
    vmem = pl.BlockSpec(memory_space=pltpu.VMEM)
    f32 = jnp.float32
    pair = pltpu.SemaphoreType.DMA((2, nc))
    return pl.pallas_call(
        functools.partial(reduce_kernel, n, nc, half, window),
        out_shape=(
            jax.ShapeDtypeStruct((half, cols), f32),
            jax.ShapeDtypeStruct((half + window, kv_cols), f32),
            jax.ShapeDtypeStruct(row_sq.shape, f32),
        ),
        in_specs=[vmem] * 3,
        out_specs=(vmem,) * 3,
        scratch_shapes=[
            pltpu.VMEM((half, cols), f32),
            pltpu.VMEM((half + window, kv_cols), f32),
            pltpu.VMEM((half, cols), f32),
            pltpu.VMEM((half, kv_cols), f32),
            pltpu.VMEM((n - 1,) + row_sq.shape, f32),
            pair,
            pair,
            pair,
            pair,
            pltpu.SemaphoreType.DMA((2, n - 1)),
        ],
        compiler_params=pltpu.CompilerParams(
            collective_id=0, has_side_effects=True, vmem_limit_bytes=40 << 20
        ),
    )(q_part, kv_part, row_sq)


def spread_kernel(n, nc, half, x_ref, o_ref, rs, ls):
    me = lax.axis_index("wa")
    last = n - 1
    right = jnp.minimum(me + 1, last)
    left = jnp.maximum(me - 1, 0)
    size = half // nc
    greet_peers(n)

    def rows(base, j):
        return pl.ds(pl.multiple_of(base + j * size, 16), size)

    def right_copy(j, first_hop):
        at = rows(0, j)
        src = x_ref if first_hop else o_ref
        return send_to(src.at[at], o_ref.at[at], rs.at[0, j], rs.at[1, j], right)

    def left_copy(j, first_hop):
        at = rows(half, j)
        src = x_ref.at[rows(0, j)] if first_hop else o_ref.at[at]
        return send_to(src, o_ref.at[at], ls.at[0, j], ls.at[1, j], left)

    @pl.loop(0, nc + last)
    def _(s):
        j = s - me
        i = s - (last - me)
        right_on = (j >= 0) & (j < nc)
        left_on = (i >= 0) & (i < nc)

        @pl.when(right_on & (me == 0))
        def _():
            right_copy(j, True).start()
            o_ref[rows(0, j), :] = x_ref[rows(0, j), :]

        @pl.when(left_on & (me == last))
        def _():
            left_copy(i, True).start()
            o_ref[rows(half, i), :] = x_ref[rows(0, i), :]

        @pl.when(right_on & (me > 0))
        def _():
            right_copy(j, False).wait_recv()

        @pl.when(right_on & (me > 0) & (me < last))
        def _():
            right_copy(j, False).start()

        @pl.when(left_on & (me < last))
        def _():
            left_copy(i, False).wait_recv()

        @pl.when(left_on & (me > 0) & (me < last))
        def _():
            left_copy(i, False).start()

    @pl.loop(0, nc)
    def _(j):
        @pl.when(me < last)
        def _():
            right_copy(j, False).wait_send()

        @pl.when(me > 0)
        def _():
            left_copy(j, False).wait_send()


def spread_from_ends(x, n):
    half, cols = x.shape
    nc = half // 16
    vmem = pl.BlockSpec(memory_space=pltpu.VMEM)
    pair = pltpu.SemaphoreType.DMA((2, nc))
    return pl.pallas_call(
        functools.partial(spread_kernel, n, nc, half),
        out_shape=jax.ShapeDtypeStruct((2 * half, cols), x.dtype),
        in_specs=[vmem],
        out_specs=vmem,
        scratch_shapes=[pair, pair],
        compiler_params=pltpu.CompilerParams(
            collective_id=1, has_side_effects=True, vmem_limit_bytes=16 << 20
        ),
    )(x)


def attend(queries, key_head, value_head, segment_ids, first):
    q_rows = queries.shape[0]
    size = min(WINDOW, q_rows)
    segment_pad = jnp.pad(segment_ids, (WINDOW, 0), constant_values=-1)
    outs = []
    for at in range(0, q_rows, size):
        start = first + at
        query = queries[at : at + size]
        key = key_head[at : at + size + WINDOW]
        value = value_head[at : at + size + WINDOW]
        k_segment = lax.dynamic_slice_in_dim(segment_pad, start, size + WINDOW, 0)
        q_segment = lax.dynamic_slice_in_dim(segment_ids, start, size, 0)
        k_at = jnp.arange(size + WINDOW, dtype=jnp.int32) - WINDOW
        q_at = jnp.arange(size, dtype=jnp.int32)
        allowed = (q_segment[:, None] == k_segment[None, :]) & (k_at[None, :] <= q_at[:, None])
        allowed = allowed & (k_at + start >= 0)[None, :]
        scores = jnp.einsum(
            "thd,sd->hts", query, key, preferred_element_type=jnp.float32
        ) * HD ** (-0.5)
        scores = jnp.where(allowed[None], scores, -1e30)
        peak = jnp.max(scores, axis=-1, keepdims=True)
        expo = jnp.where(allowed[None], jnp.exp(scores - peak), 0.0)
        weights = (expo / jnp.sum(expo, axis=-1, keepdims=True)).astype(jnp.bfloat16)
        out = jnp.einsum("hts,sd->thd", weights, value, preferred_element_type=jnp.float32)
        outs.append(out.astype(jnp.bfloat16))
    return jnp.concatenate(outs, axis=0)


def on_device(tokens, gain_attn, w_query, w_key, w_value, w_out, gain_ffn, segment_ids):
    rows_dev, width_dev = tokens.shape
    n_wa = lax.axis_size("wa")
    n_ha = lax.axis_size("ha")
    total = rows_dev * n_ha
    width = width_dev * n_wa
    head_cols = w_query.shape[1]
    heads_dev = head_cols // HD
    token_f = tokens.astype(jnp.float32)
    gain_one = gain_attn.astype(jnp.float32)
    kv_head = lax.axis_index("ha") // (n_ha // KVH)
    kv_weights = jnp.concatenate(
        [
            lax.dynamic_slice_in_dim(w_key, kv_head * HD, HD, 1),
            lax.dynamic_slice_in_dim(w_value, kv_head * HD, HD, 1),
        ],
        axis=1,
    )
    gathered = lax.all_gather(tokens, "ha", axis=0, tiled=True)
    gathered_f = gathered.astype(jnp.float32)
    row_sq = jnp.sum(gathered_f * gathered_f, axis=1)
    scaled = (gathered_f * gain_one).astype(jnp.bfloat16)
    kv_part = jnp.dot(scaled, kv_weights, preferred_element_type=jnp.float32)
    q_part = jnp.dot(scaled, w_query, preferred_element_type=jnp.float32)
    lanes = min(total, 128)
    query_f, kv_sum, sq_sum = reduce_to_ends(
        q_part, kv_part, row_sq.reshape(total // lanes, lanes), n_wa, WINDOW
    )
    row_scale = lax.rsqrt(sq_sum.reshape(total) / width + EPS)
    q_rows = total // 2
    first = jnp.where(lax.axis_index("wa") == n_wa - 1, q_rows, 0)
    kv_rows = q_rows + WINDOW

    def around(table):
        padded = jnp.pad(table, ((WINDOW, 0),) + ((0, 0),) * (table.ndim - 1))
        return lax.dynamic_slice_in_dim(padded, first, kv_rows, 0)

    index_all = jnp.arange(total, dtype=jnp.int32)
    fresh = jnp.concatenate([jnp.ones((1,), dtype=bool), segment_ids[1:] != segment_ids[:-1]])
    start_all = lax.cummax(jnp.where(fresh, index_all, jnp.zeros_like(index_all)), axis=0)
    cosine, sine = rope_tables((index_all - start_all).astype(jnp.float32))
    scale = around(row_scale)
    cosine, sine = around(cosine), around(sine)
    key_plain = (kv_sum[:, :HD] * scale[:, None]).astype(jnp.bfloat16)
    key_plain = lax.optimization_barrier(key_plain)
    value_head = (kv_sum[:, HD:] * scale[:, None]).astype(jnp.bfloat16)
    key_head = rotate(key_plain.astype(jnp.float32).reshape(kv_rows, 1, HD), cosine, sine)
    key_head = key_head.reshape(kv_rows, HD).astype(jnp.bfloat16)
    q_scale, q_cos, q_sin = scale[WINDOW:], cosine[WINDOW:], sine[WINDOW:]
    queries = rotate(
        (query_f * q_scale[:, None]).reshape(q_rows, heads_dev, HD), q_cos, q_sin
    ).astype(jnp.bfloat16)
    head_out = attend(queries, key_head, value_head, segment_ids, first)
    head_out = head_out.reshape(q_rows, head_cols)
    head_all = spread_from_ends(head_out, n_wa)
    block = head_all
    attended = lax.psum_scatter(
        jnp.dot(block, w_out, preferred_element_type=jnp.float32).astype(jnp.bfloat16),
        "ha",
        scatter_dimension=0,
        tiled=True,
    )
    residual_out = (token_f + attended.astype(jnp.float32)).astype(jnp.bfloat16)
    residual_f = residual_out.astype(jnp.float32)
    own_two = jnp.sum(residual_f * residual_f, axis=1)
    own_two = jnp.pad(own_two, (0, -rows_dev % 128)).reshape(-1, 128)
    square_two = peer_sum(own_two, n_wa).reshape(-1)[:rows_dev]
    scale_two = lax.rsqrt(square_two / width + EPS)
    ffn_input = (residual_f * scale_two[:, None] * gain_ffn.astype(jnp.float32)).astype(
        jnp.bfloat16
    )
    return (residual_out, ffn_input)


def solution(mesh):
    in_specs = (
        P("ha", "wa"),
        P("wa"),
        P("wa", "ha"),
        P("wa", None),
        P("wa", None),
        P("ha", "wa"),
        P("wa"),
        P(),
    )
    out_specs = (P("ha", "wa"), P("ha", "wa"))
    return jax.shard_map(
        on_device, mesh=mesh, in_specs=in_specs, out_specs=out_specs, check_vma=False
    )
```

```python
import functools

import jax
import jax.numpy as jnp
from jax import lax
from jax.experimental import pallas as pl
from jax.experimental.pallas import tpu as pltpu
from jax.sharding import PartitionSpec as P

KVH = 8
HD = 128
WINDOW = 256


EPS = 1e-05


def rope_tables(position):
    half = HD // 2
    inverse = 500000.0 ** (-(jnp.arange(half, dtype=jnp.float32) * 2.0 / HD))
    angle = position[:, None] * inverse[None, :]
    return (jnp.cos(angle), jnp.sin(angle))


def rotate(values, cosine, sine):
    half = values.shape[-1] // 2
    first = values[..., :half]
    second = values[..., half:]
    cosine = cosine[:, None, :]
    sine = sine[:, None, :]
    return jnp.concatenate(
        [first * cosine - second * sine, second * cosine + first * sine], axis=-1
    )


SKEW = 3


def greet_peers(n):
    me = lax.axis_index("wa")
    barrier = pltpu.get_barrier_semaphore()
    for d in range(1, n):
        pl.semaphore_signal(
            barrier,
            inc=1,
            device_id={"wa": lax.rem(me + d, n)},
            device_id_type=pl.DeviceIdType.MESH,
        )
    pl.semaphore_wait(barrier, n - 1)


def send_to(src, dst, send_sem, recv_sem, peer):
    return pltpu.make_async_remote_copy(
        src_ref=src,
        dst_ref=dst,
        send_sem=send_sem,
        recv_sem=recv_sem,
        device_id={"wa": peer},
        device_id_type=pl.DeviceIdType.MESH,
    )


def peer_copies(n, x_ref, land, sems):
    me = lax.axis_index("wa")
    return [
        send_to(x_ref, land.at[d - 1], sems.at[0, d - 1], sems.at[1, d - 1], lax.rem(me + d, n))
        for d in range(1, n)
    ]


def peer_sum_kernel(n, x_ref, o_ref, land, sems):
    greet_peers(n)
    copies = peer_copies(n, x_ref, land, sems)
    for copy in copies:
        copy.start()
    for copy in copies:
        copy.wait()
    total = x_ref[...]
    for d in range(n - 1):
        total = total + land[d]
    o_ref[...] = total


def peer_sum(x, n):
    vmem = pl.BlockSpec(memory_space=pltpu.VMEM)
    return pl.pallas_call(
        functools.partial(peer_sum_kernel, n),
        out_shape=jax.ShapeDtypeStruct(x.shape, x.dtype),
        in_specs=[vmem],
        out_specs=vmem,
        scratch_shapes=[
            pltpu.VMEM((n - 1,) + x.shape, x.dtype),
            pltpu.SemaphoreType.DMA((2, n - 1)),
        ],
        compiler_params=pltpu.CompilerParams(
            collective_id=2, has_side_effects=True, vmem_limit_bytes=4 << 20
        ),
    )(x)


def reduce_kernel(
    n, nc, half, window, q_ref, kv_ref, sq_ref, qo, kvo, sqo,
    rq, rkv, lq, lkv, lsq, rqs, rks, lqs, lks, sqs,
):
    me = lax.axis_index("wa")
    last = n - 1
    right = jnp.minimum(me + 1, last)
    left = jnp.maximum(me - 1, 0)
    cq = half // nc
    cw = (half + window) // nc
    greet_peers(n)
    small = peer_copies(n, sq_ref, lsq, sqs)
    for copy in small:
        copy.start()
    kvo[pl.ds(0, window), :] = jnp.zeros((window, kvo.shape[1]), kvo.dtype)

    def rows(base, j, size):
        return pl.ds(pl.multiple_of(base + j * size, 8), size)

    def right_copy(j, first_hop):
        own, wide = rows(0, j, cq), rows(0, j, cw)
        if first_hop:
            src, src_kv = q_ref.at[rows(half, j, cq)], kv_ref.at[rows(half - window, j, cw)]
        else:
            src, src_kv = rq.at[own], rkv.at[wide]
        return (
            send_to(src, rq.at[own], rqs.at[0, j], rqs.at[1, j], right),
            send_to(src_kv, rkv.at[wide], rks.at[0, j], rks.at[1, j], right),
        )

    def left_copy(j, first_hop):
        own = rows(0, j, cq)
        src, src_kv = (q_ref, kv_ref) if first_hop else (lq, lkv)
        return (
            send_to(src.at[own], lq.at[own], lqs.at[0, j], lqs.at[1, j], left),
            send_to(src_kv.at[own], lkv.at[own], lks.at[0, j], lks.at[1, j], left),
        )

    @pl.loop(0, nc + SKEW * last)
    def _(s):
        j = s - SKEW * me
        i = s - SKEW * (last - me)
        right_on = (j >= 0) & (j < nc)
        left_on = (i >= 0) & (i < nc)

        @pl.when(right_on & (me > 0))
        def _():
            for copy in right_copy(j, False):
                copy.wait_recv()
            own, wide = rows(0, j, cq), rows(0, j, cw)
            rq[own, :] = rq[own, :] + q_ref[rows(half, j, cq), :]
            rkv[wide, :] = rkv[wide, :] + kv_ref[rows(half - window, j, cw), :]

        @pl.when(left_on & (me < last))
        def _():
            for copy in left_copy(i, False):
                copy.wait_recv()
            own = rows(0, i, cq)
            lq[own, :] = lq[own, :] + q_ref[own, :]
            lkv[own, :] = lkv[own, :] + kv_ref[own, :]

        @pl.when(right_on & (me == 0))
        def _():
            for copy in right_copy(j, True):
                copy.start()

        @pl.when(left_on & (me == last))
        def _():
            for copy in left_copy(i, True):
                copy.start()

        @pl.when(right_on & (me > 0) & (me < last))
        def _():
            for copy in right_copy(j, False):
                copy.start()

        @pl.when(left_on & (me > 0) & (me < last))
        def _():
            for copy in left_copy(i, False):
                copy.start()

        @pl.when(right_on & (me == last))
        def _():
            own, wide = rows(0, j, cq), rows(0, j, cw)
            qo[own, :] = rq[own, :]
            kvo[wide, :] = rkv[wide, :]

        @pl.when(left_on & (me < last))
        def _():
            own = rows(0, i, cq)
            qo[own, :] = lq[own, :]
            kvo[rows(window, i, cq), :] = lkv[own, :]

    @pl.loop(0, nc)
    def _(j):
        @pl.when(me < last)
        def _():
            for copy in right_copy(j, False):
                copy.wait_send()

        @pl.when(me > 0)
        def _():
            for copy in left_copy(j, False):
                copy.wait_send()

    for copy in small:
        copy.wait()
    total = sq_ref[...]
    for d in range(n - 1):
        total = total + lsq[d]
    sqo[...] = total


def reduce_to_ends(q_part, kv_part, row_sq, n, window):
    rows, cols = q_part.shape
    kv_cols = kv_part.shape[1]
    half = rows // 2
    nc = half // 16
    vmem = pl.BlockSpec(memory_space=pltpu.VMEM)
    f32 = jnp.float32
    pair = pltpu.SemaphoreType.DMA((2, nc))
    return pl.pallas_call(
        functools.partial(reduce_kernel, n, nc, half, window),
        out_shape=(
            jax.ShapeDtypeStruct((half, cols), f32),
            jax.ShapeDtypeStruct((half + window, kv_cols), f32),
            jax.ShapeDtypeStruct(row_sq.shape, f32),
        ),
        in_specs=[vmem] * 3,
        out_specs=(vmem,) * 3,
        scratch_shapes=[
            pltpu.VMEM((half, cols), f32),
            pltpu.VMEM((half + window, kv_cols), f32),
            pltpu.VMEM((half, cols), f32),
            pltpu.VMEM((half, kv_cols), f32),
            pltpu.VMEM((n - 1,) + row_sq.shape, f32),
            pair,
            pair,
            pair,
            pair,
            pltpu.SemaphoreType.DMA((2, n - 1)),
        ],
        compiler_params=pltpu.CompilerParams(
            collective_id=0, has_side_effects=True, vmem_limit_bytes=40 << 20
        ),
    )(q_part, kv_part, row_sq)


def spread_kernel(n, nc, half, x_ref, o_ref, rs, ls):
    me = lax.axis_index("wa")
    last = n - 1
    right = jnp.minimum(me + 1, last)
    left = jnp.maximum(me - 1, 0)
    size = half // nc
    greet_peers(n)

    def rows(base, j):
        return pl.ds(pl.multiple_of(base + j * size, 16), size)

    def right_copy(j, first_hop):
        at = rows(0, j)
        src = x_ref if first_hop else o_ref
        return send_to(src.at[at], o_ref.at[at], rs.at[0, j], rs.at[1, j], right)

    def left_copy(j, first_hop):
        at = rows(half, j)
        src = x_ref.at[rows(0, j)] if first_hop else o_ref.at[at]
        return send_to(src, o_ref.at[at], ls.at[0, j], ls.at[1, j], left)

    @pl.loop(0, nc + SKEW * last)
    def _(s):
        j = s - SKEW * me
        i = s - SKEW * (last - me)
        right_on = (j >= 0) & (j < nc)
        left_on = (i >= 0) & (i < nc)

        @pl.when(right_on & (me == 0))
        def _():
            right_copy(j, True).start()
            o_ref[rows(0, j), :] = x_ref[rows(0, j), :]

        @pl.when(left_on & (me == last))
        def _():
            left_copy(i, True).start()
            o_ref[rows(half, i), :] = x_ref[rows(0, i), :]

        @pl.when(right_on & (me > 0))
        def _():
            right_copy(j, False).wait_recv()

        @pl.when(right_on & (me > 0) & (me < last))
        def _():
            right_copy(j, False).start()

        @pl.when(left_on & (me < last))
        def _():
            left_copy(i, False).wait_recv()

        @pl.when(left_on & (me > 0) & (me < last))
        def _():
            left_copy(i, False).start()

    @pl.loop(0, nc)
    def _(j):
        @pl.when(me < last)
        def _():
            right_copy(j, False).wait_send()

        @pl.when(me > 0)
        def _():
            left_copy(j, False).wait_send()


def spread_from_ends(x, n):
    half, cols = x.shape
    nc = half // 16
    vmem = pl.BlockSpec(memory_space=pltpu.VMEM)
    pair = pltpu.SemaphoreType.DMA((2, nc))
    return pl.pallas_call(
        functools.partial(spread_kernel, n, nc, half),
        out_shape=jax.ShapeDtypeStruct((2 * half, cols), x.dtype),
        in_specs=[vmem],
        out_specs=vmem,
        scratch_shapes=[pair, pair],
        compiler_params=pltpu.CompilerParams(
            collective_id=1, has_side_effects=True, vmem_limit_bytes=16 << 20
        ),
    )(x)


def attend(queries, key_head, value_head, segment_ids, first):
    q_rows = queries.shape[0]
    size = min(WINDOW, q_rows)
    segment_pad = jnp.pad(segment_ids, (WINDOW, 0), constant_values=-1)
    outs = []
    for at in range(0, q_rows, size):
        start = first + at
        query = queries[at : at + size]
        key = key_head[at : at + size + WINDOW]
        value = value_head[at : at + size + WINDOW]
        k_segment = lax.dynamic_slice_in_dim(segment_pad, start, size + WINDOW, 0)
        q_segment = lax.dynamic_slice_in_dim(segment_ids, start, size, 0)
        k_at = jnp.arange(size + WINDOW, dtype=jnp.int32) - WINDOW
        q_at = jnp.arange(size, dtype=jnp.int32)
        allowed = (q_segment[:, None] == k_segment[None, :]) & (k_at[None, :] <= q_at[:, None])
        allowed = allowed & (k_at + start >= 0)[None, :]
        scores = jnp.einsum(
            "thd,sd->hts", query, key, preferred_element_type=jnp.float32
        ) * HD ** (-0.5)
        scores = jnp.where(allowed[None], scores, -1e30)
        peak = jnp.max(scores, axis=-1, keepdims=True)
        expo = jnp.where(allowed[None], jnp.exp(scores - peak), 0.0)
        weights = (expo / jnp.sum(expo, axis=-1, keepdims=True)).astype(jnp.bfloat16)
        out = jnp.einsum("hts,sd->thd", weights, value, preferred_element_type=jnp.float32)
        outs.append(out.astype(jnp.bfloat16))
    return jnp.concatenate(outs, axis=0)


def on_device(tokens, gain_attn, w_query, w_key, w_value, w_out, gain_ffn, segment_ids):
    rows_dev, width_dev = tokens.shape
    n_wa = lax.axis_size("wa")
    n_ha = lax.axis_size("ha")
    total = rows_dev * n_ha
    width = width_dev * n_wa
    head_cols = w_query.shape[1]
    heads_dev = head_cols // HD
    token_f = tokens.astype(jnp.float32)
    gain_one = gain_attn.astype(jnp.float32)
    kv_head = lax.axis_index("ha") // (n_ha // KVH)
    kv_weights = jnp.concatenate(
        [
            lax.dynamic_slice_in_dim(w_key, kv_head * HD, HD, 1),
            lax.dynamic_slice_in_dim(w_value, kv_head * HD, HD, 1),
        ],
        axis=1,
    )
    deep = width_dev // 2
    q_part = kv_part = row_sq = 0.0
    for at in range(0, width_dev, deep):
        part = slice(at, at + deep)
        gathered = lax.all_gather(tokens[:, part], "ha", axis=0, tiled=True)
        if at:
            gathered, q_part = lax.optimization_barrier((gathered, q_part))
        gathered_f = gathered.astype(jnp.float32)
        row_sq = row_sq + jnp.sum(gathered_f * gathered_f, axis=1)
        scaled = (gathered_f * gain_one[part]).astype(jnp.bfloat16)
        kv_part = kv_part + jnp.dot(
            scaled, kv_weights[part], preferred_element_type=jnp.float32
        )
        q_part = q_part + jnp.dot(scaled, w_query[part], preferred_element_type=jnp.float32)
    lanes = min(total, 128)
    query_f, kv_sum, sq_sum = reduce_to_ends(
        q_part, kv_part, row_sq.reshape(total // lanes, lanes), n_wa, WINDOW
    )
    row_scale = lax.rsqrt(sq_sum.reshape(total) / width + EPS)
    q_rows = total // 2
    first = jnp.where(lax.axis_index("wa") == n_wa - 1, q_rows, 0)
    kv_rows = q_rows + WINDOW

    def around(table):
        padded = jnp.pad(table, ((WINDOW, 0),) + ((0, 0),) * (table.ndim - 1))
        return lax.dynamic_slice_in_dim(padded, first, kv_rows, 0)

    index_all = jnp.arange(total, dtype=jnp.int32)
    fresh = jnp.concatenate([jnp.ones((1,), dtype=bool), segment_ids[1:] != segment_ids[:-1]])
    start_all = lax.cummax(jnp.where(fresh, index_all, jnp.zeros_like(index_all)), axis=0)
    cosine, sine = rope_tables((index_all - start_all).astype(jnp.float32))
    scale = around(row_scale)
    cosine, sine = around(cosine), around(sine)
    key_plain = (kv_sum[:, :HD] * scale[:, None]).astype(jnp.bfloat16)
    key_plain = lax.optimization_barrier(key_plain)
    value_head = (kv_sum[:, HD:] * scale[:, None]).astype(jnp.bfloat16)
    key_head = rotate(key_plain.astype(jnp.float32).reshape(kv_rows, 1, HD), cosine, sine)
    key_head = key_head.reshape(kv_rows, HD).astype(jnp.bfloat16)
    q_scale, q_cos, q_sin = scale[WINDOW:], cosine[WINDOW:], sine[WINDOW:]
    queries = rotate(
        (query_f * q_scale[:, None]).reshape(q_rows, heads_dev, HD), q_cos, q_sin
    ).astype(jnp.bfloat16)
    head_out = attend(queries, key_head, value_head, segment_ids, first)
    head_out = head_out.reshape(q_rows, head_cols)
    head_all = spread_from_ends(head_out, n_wa)
    col = width_dev // 2
    attended = jnp.concatenate(
        [
            lax.psum_scatter(
                jnp.dot(
                    head_all, w_out[:, at : at + col], preferred_element_type=jnp.float32
                ).astype(jnp.bfloat16),
                "ha",
                scatter_dimension=0,
                tiled=True,
            )
            for at in range(0, width_dev, col)
        ],
        axis=1,
    )
    residual_out = (token_f + attended.astype(jnp.float32)).astype(jnp.bfloat16)
    residual_f = residual_out.astype(jnp.float32)
    own_two = jnp.sum(residual_f * residual_f, axis=1)
    own_two = jnp.pad(own_two, (0, -rows_dev % 128)).reshape(-1, 128)
    square_two = peer_sum(own_two, n_wa).reshape(-1)[:rows_dev]
    scale_two = lax.rsqrt(square_two / width + EPS)
    ffn_input = (residual_f * scale_two[:, None] * gain_ffn.astype(jnp.float32)).astype(
        jnp.bfloat16
    )
    return (residual_out, ffn_input)


def solution(mesh):
    in_specs = (
        P("ha", "wa"),
        P("wa"),
        P("wa", "ha"),
        P("wa", None),
        P("wa", None),
        P("ha", "wa"),
        P("wa"),
        P(),
    )
    out_specs = (P("ha", "wa"), P("ha", "wa"))
    return jax.shard_map(
        on_device, mesh=mesh, in_specs=in_specs, out_specs=out_specs, check_vma=False
    )
```

```python
import functools

import jax
import jax.numpy as jnp
from jax import lax
from jax.experimental import pallas as pl
from jax.experimental.pallas import tpu as pltpu
from jax.sharding import PartitionSpec as P

KVH = 8
HD = 128
WINDOW = 256


EPS = 1e-05


def rope_tables(position):
    half = HD // 2
    inverse = 500000.0 ** (-(jnp.arange(half, dtype=jnp.float32) * 2.0 / HD))
    angle = position[:, None] * inverse[None, :]
    return (jnp.cos(angle), jnp.sin(angle))


def rotate(values, cosine, sine):
    half = values.shape[-1] // 2
    first = values[..., :half]
    second = values[..., half:]
    cosine = cosine[:, None, :]
    sine = sine[:, None, :]
    return jnp.concatenate(
        [first * cosine - second * sine, second * cosine + first * sine], axis=-1
    )


SKEW = 3


def greet_peers(n):
    me = lax.axis_index("wa")
    barrier = pltpu.get_barrier_semaphore()
    for d in range(1, n):
        pl.semaphore_signal(
            barrier,
            inc=1,
            device_id={"wa": lax.rem(me + d, n)},
            device_id_type=pl.DeviceIdType.MESH,
        )
    pl.semaphore_wait(barrier, n - 1)


def send_to(src, dst, send_sem, recv_sem, peer):
    return pltpu.make_async_remote_copy(
        src_ref=src,
        dst_ref=dst,
        send_sem=send_sem,
        recv_sem=recv_sem,
        device_id={"wa": peer},
        device_id_type=pl.DeviceIdType.MESH,
    )


def peer_copies(n, x_ref, land, sems):
    me = lax.axis_index("wa")
    return [
        send_to(x_ref, land.at[d - 1], sems.at[0, d - 1], sems.at[1, d - 1], lax.rem(me + d, n))
        for d in range(1, n)
    ]


def peer_sum_kernel(n, x_ref, o_ref, land, sems):
    greet_peers(n)
    copies = peer_copies(n, x_ref, land, sems)
    for copy in copies:
        copy.start()
    for copy in copies:
        copy.wait()
    total = x_ref[...]
    for d in range(n - 1):
        total = total + land[d]
    o_ref[...] = total


def peer_sum(x, n):
    vmem = pl.BlockSpec(memory_space=pltpu.VMEM)
    return pl.pallas_call(
        functools.partial(peer_sum_kernel, n),
        out_shape=jax.ShapeDtypeStruct(x.shape, x.dtype),
        in_specs=[vmem],
        out_specs=vmem,
        scratch_shapes=[
            pltpu.VMEM((n - 1,) + x.shape, x.dtype),
            pltpu.SemaphoreType.DMA((2, n - 1)),
        ],
        compiler_params=pltpu.CompilerParams(
            collective_id=2, has_side_effects=True, vmem_limit_bytes=4 << 20
        ),
    )(x)


def reduce_kernel(
    n, nc, half, window, q_ref, kv_ref, sq_ref, qo, kvo, sqo,
    rq, rkv, lq, lkv, lsq, rqs, rks, lqs, lks, sqs,
):
    me = lax.axis_index("wa")
    last = n - 1
    right = jnp.minimum(me + 1, last)
    left = jnp.maximum(me - 1, 0)
    cq = half // nc
    cw = (half + window) // nc
    greet_peers(n)
    small = peer_copies(n, sq_ref, lsq, sqs)
    for copy in small:
        copy.start()
    kvo[pl.ds(0, window), :] = jnp.zeros((window, kvo.shape[1]), kvo.dtype)

    def rows(base, j, size):
        return pl.ds(pl.multiple_of(base + j * size, 8), size)

    def right_copy(j, first_hop):
        own, wide = rows(0, j, cq), rows(0, j, cw)
        if first_hop:
            src, src_kv = q_ref.at[rows(half, j, cq)], kv_ref.at[rows(half - window, j, cw)]
        else:
            src, src_kv = rq.at[own], rkv.at[wide]
        return (
            send_to(src, rq.at[own], rqs.at[0, j], rqs.at[1, j], right),
            send_to(src_kv, rkv.at[wide], rks.at[0, j], rks.at[1, j], right),
        )

    def left_copy(j, first_hop):
        own = rows(0, j, cq)
        src, src_kv = (q_ref, kv_ref) if first_hop else (lq, lkv)
        return (
            send_to(src.at[own], lq.at[own], lqs.at[0, j], lqs.at[1, j], left),
            send_to(src_kv.at[own], lkv.at[own], lks.at[0, j], lks.at[1, j], left),
        )

    @pl.loop(0, nc + SKEW * last)
    def _(s):
        j = s - SKEW * me
        i = s - SKEW * (last - me)
        right_on = (j >= 0) & (j < nc)
        left_on = (i >= 0) & (i < nc)

        @pl.when(right_on & (me > 0))
        def _():
            for copy in right_copy(j, False):
                copy.wait_recv()
            own, wide = rows(0, j, cq), rows(0, j, cw)
            rq[own, :] = rq[own, :] + q_ref[rows(half, j, cq), :]
            rkv[wide, :] = rkv[wide, :] + kv_ref[rows(half - window, j, cw), :]

        @pl.when(left_on & (me < last))
        def _():
            for copy in left_copy(i, False):
                copy.wait_recv()
            own = rows(0, i, cq)
            lq[own, :] = lq[own, :] + q_ref[own, :]
            lkv[own, :] = lkv[own, :] + kv_ref[own, :]

        @pl.when(right_on & (me == 0))
        def _():
            for copy in right_copy(j, True):
                copy.start()

        @pl.when(left_on & (me == last))
        def _():
            for copy in left_copy(i, True):
                copy.start()

        @pl.when(right_on & (me > 0) & (me < last))
        def _():
            for copy in right_copy(j, False):
                copy.start()

        @pl.when(left_on & (me > 0) & (me < last))
        def _():
            for copy in left_copy(i, False):
                copy.start()

        @pl.when(right_on & (me == last))
        def _():
            own, wide = rows(0, j, cq), rows(0, j, cw)
            qo[own, :] = rq[own, :]
            kvo[wide, :] = rkv[wide, :]

        @pl.when(left_on & (me < last))
        def _():
            own = rows(0, i, cq)
            qo[own, :] = lq[own, :]
            kvo[rows(window, i, cq), :] = lkv[own, :]

    @pl.loop(0, nc)
    def _(j):
        @pl.when(me < last)
        def _():
            for copy in right_copy(j, False):
                copy.wait_send()

        @pl.when(me > 0)
        def _():
            for copy in left_copy(j, False):
                copy.wait_send()

    for copy in small:
        copy.wait()
    total = sq_ref[...]
    for d in range(n - 1):
        total = total + lsq[d]
    sqo[...] = total


def reduce_to_ends(q_part, kv_part, row_sq, n, window):
    rows, cols = q_part.shape
    kv_cols = kv_part.shape[1]
    half = rows // 2
    nc = half // 16
    vmem = pl.BlockSpec(memory_space=pltpu.VMEM)
    f32 = jnp.float32
    pair = pltpu.SemaphoreType.DMA((2, nc))
    return pl.pallas_call(
        functools.partial(reduce_kernel, n, nc, half, window),
        out_shape=(
            jax.ShapeDtypeStruct((half, cols), f32),
            jax.ShapeDtypeStruct((half + window, kv_cols), f32),
            jax.ShapeDtypeStruct(row_sq.shape, f32),
        ),
        in_specs=[vmem] * 3,
        out_specs=(vmem,) * 3,
        scratch_shapes=[
            pltpu.VMEM((half, cols), f32),
            pltpu.VMEM((half + window, kv_cols), f32),
            pltpu.VMEM((half, cols), f32),
            pltpu.VMEM((half, kv_cols), f32),
            pltpu.VMEM((n - 1,) + row_sq.shape, f32),
            pair,
            pair,
            pair,
            pair,
            pltpu.SemaphoreType.DMA((2, n - 1)),
        ],
        compiler_params=pltpu.CompilerParams(
            collective_id=0, has_side_effects=True, vmem_limit_bytes=40 << 20
        ),
    )(q_part, kv_part, row_sq)


def spread_kernel(n, nc, half, x_ref, o_ref, rs, ls):
    me = lax.axis_index("wa")
    last = n - 1
    right = jnp.minimum(me + 1, last)
    left = jnp.maximum(me - 1, 0)
    size = half // nc
    greet_peers(n)

    def rows(base, j):
        return pl.ds(pl.multiple_of(base + j * size, 16), size)

    def right_copy(j, first_hop):
        at = rows(0, j)
        src = x_ref if first_hop else o_ref
        return send_to(src.at[at], o_ref.at[at], rs.at[0, j], rs.at[1, j], right)

    def left_copy(j, first_hop):
        at = rows(half, j)
        src = x_ref.at[rows(0, j)] if first_hop else o_ref.at[at]
        return send_to(src, o_ref.at[at], ls.at[0, j], ls.at[1, j], left)

    @pl.loop(0, nc + SKEW * last)
    def _(s):
        j = s - SKEW * me
        i = s - SKEW * (last - me)
        right_on = (j >= 0) & (j < nc)
        left_on = (i >= 0) & (i < nc)

        @pl.when(right_on & (me == 0))
        def _():
            right_copy(j, True).start()
            o_ref[rows(0, j), :] = x_ref[rows(0, j), :]

        @pl.when(left_on & (me == last))
        def _():
            left_copy(i, True).start()
            o_ref[rows(half, i), :] = x_ref[rows(0, i), :]

        @pl.when(right_on & (me > 0))
        def _():
            right_copy(j, False).wait_recv()

        @pl.when(right_on & (me > 0) & (me < last))
        def _():
            right_copy(j, False).start()

        @pl.when(left_on & (me < last))
        def _():
            left_copy(i, False).wait_recv()

        @pl.when(left_on & (me > 0) & (me < last))
        def _():
            left_copy(i, False).start()

    @pl.loop(0, nc)
    def _(j):
        @pl.when(me < last)
        def _():
            right_copy(j, False).wait_send()

        @pl.when(me > 0)
        def _():
            left_copy(j, False).wait_send()


def spread_from_ends(x, n):
    half, cols = x.shape
    nc = half // 16
    vmem = pl.BlockSpec(memory_space=pltpu.VMEM)
    pair = pltpu.SemaphoreType.DMA((2, nc))
    return pl.pallas_call(
        functools.partial(spread_kernel, n, nc, half),
        out_shape=jax.ShapeDtypeStruct((2 * half, cols), x.dtype),
        in_specs=[vmem],
        out_specs=vmem,
        scratch_shapes=[pair, pair],
        compiler_params=pltpu.CompilerParams(
            collective_id=1, has_side_effects=True, vmem_limit_bytes=16 << 20
        ),
    )(x)


def attend(queries, key_head, value_head, segment_ids, first):
    q_rows = queries.shape[0]
    size = min(WINDOW, q_rows)
    segment_pad = jnp.pad(segment_ids, (WINDOW, 0), constant_values=-1)
    outs = []
    for at in range(0, q_rows, size):
        start = first + at
        query = queries[at : at + size]
        key = key_head[at : at + size + WINDOW]
        value = value_head[at : at + size + WINDOW]
        k_segment = lax.dynamic_slice_in_dim(segment_pad, start, size + WINDOW, 0)
        q_segment = lax.dynamic_slice_in_dim(segment_ids, start, size, 0)
        k_at = jnp.arange(size + WINDOW, dtype=jnp.int32) - WINDOW
        q_at = jnp.arange(size, dtype=jnp.int32)
        allowed = (q_segment[:, None] == k_segment[None, :]) & (k_at[None, :] <= q_at[:, None])
        allowed = allowed & (k_at + start >= 0)[None, :]
        scores = jnp.einsum(
            "thd,sd->hts", query, key, preferred_element_type=jnp.float32
        ) * HD ** (-0.5)
        scores = jnp.where(allowed[None], scores, -1e30)
        peak = jnp.max(scores, axis=-1, keepdims=True)
        expo = jnp.where(allowed[None], jnp.exp(scores - peak), 0.0)
        weights = (expo / jnp.sum(expo, axis=-1, keepdims=True)).astype(jnp.bfloat16)
        out = jnp.einsum("hts,sd->thd", weights, value, preferred_element_type=jnp.float32)
        outs.append(out.astype(jnp.bfloat16))
    return jnp.concatenate(outs, axis=0)


def on_device(tokens, gain_attn, w_query, w_key, w_value, w_out, gain_ffn, segment_ids):
    rows_dev, width_dev = tokens.shape
    n_wa = lax.axis_size("wa")
    n_ha = lax.axis_size("ha")
    total = rows_dev * n_ha
    width = width_dev * n_wa
    head_cols = w_query.shape[1]
    heads_dev = head_cols // HD
    token_f = tokens.astype(jnp.float32)
    gain_one = gain_attn.astype(jnp.float32)
    kv_head = lax.axis_index("ha") // (n_ha // KVH)
    kv_weights = jnp.concatenate(
        [
            lax.dynamic_slice_in_dim(w_key, kv_head * HD, HD, 1),
            lax.dynamic_slice_in_dim(w_value, kv_head * HD, HD, 1),
        ],
        axis=1,
    )
    gathered = lax.all_gather(tokens, "ha", axis=0, tiled=True)
    gathered_f = gathered.astype(jnp.float32)
    row_sq = jnp.sum(gathered_f * gathered_f, axis=1)
    scaled = (gathered_f * gain_one).astype(jnp.bfloat16)
    kv_part = jnp.dot(scaled, kv_weights, preferred_element_type=jnp.float32)
    q_part = jnp.dot(scaled, w_query, preferred_element_type=jnp.float32)
    lanes = min(total, 128)
    query_f, kv_sum, sq_sum = reduce_to_ends(
        q_part, kv_part, row_sq.reshape(total // lanes, lanes), n_wa, WINDOW
    )
    row_scale = lax.rsqrt(sq_sum.reshape(total) / width + EPS)
    q_rows = total // 2
    first = jnp.where(lax.axis_index("wa") == n_wa - 1, q_rows, 0)
    kv_rows = q_rows + WINDOW

    def around(table):
        padded = jnp.pad(table, ((WINDOW, 0),) + ((0, 0),) * (table.ndim - 1))
        return lax.dynamic_slice_in_dim(padded, first, kv_rows, 0)

    index_all = jnp.arange(total, dtype=jnp.int32)
    fresh = jnp.concatenate([jnp.ones((1,), dtype=bool), segment_ids[1:] != segment_ids[:-1]])
    start_all = lax.cummax(jnp.where(fresh, index_all, jnp.zeros_like(index_all)), axis=0)
    cosine, sine = rope_tables((index_all - start_all).astype(jnp.float32))
    scale = around(row_scale)
    cosine, sine = around(cosine), around(sine)
    key_plain = (kv_sum[:, :HD] * scale[:, None]).astype(jnp.bfloat16)
    key_plain = lax.optimization_barrier(key_plain)
    value_head = (kv_sum[:, HD:] * scale[:, None]).astype(jnp.bfloat16)
    key_head = rotate(key_plain.astype(jnp.float32).reshape(kv_rows, 1, HD), cosine, sine)
    key_head = key_head.reshape(kv_rows, HD).astype(jnp.bfloat16)
    q_scale, q_cos, q_sin = scale[WINDOW:], cosine[WINDOW:], sine[WINDOW:]
    queries = rotate(
        (query_f * q_scale[:, None]).reshape(q_rows, heads_dev, HD), q_cos, q_sin
    ).astype(jnp.bfloat16)
    head_out = attend(queries, key_head, value_head, segment_ids, first)
    head_out = head_out.reshape(q_rows, head_cols)
    head_all = spread_from_ends(head_out, n_wa)
    block = head_all
    attended = lax.psum_scatter(
        jnp.dot(block, w_out, preferred_element_type=jnp.float32).astype(jnp.bfloat16),
        "ha",
        scatter_dimension=0,
        tiled=True,
    )
    residual_out = (token_f + attended.astype(jnp.float32)).astype(jnp.bfloat16)
    residual_f = residual_out.astype(jnp.float32)
    own_two = jnp.sum(residual_f * residual_f, axis=1)
    own_two = jnp.pad(own_two, (0, -rows_dev % 128)).reshape(-1, 128)
    square_two = peer_sum(own_two, n_wa).reshape(-1)[:rows_dev]
    scale_two = lax.rsqrt(square_two / width + EPS)
    ffn_input = (residual_f * scale_two[:, None] * gain_ffn.astype(jnp.float32)).astype(
        jnp.bfloat16
    )
    return (residual_out, ffn_input)


def solution(mesh):
    in_specs = (
        P("ha", "wa"),
        P("wa"),
        P("wa", "ha"),
        P("wa", None),
        P("wa", None),
        P("ha", "wa"),
        P("wa"),
        P(),
    )
    out_specs = (P("ha", "wa"), P("ha", "wa"))
    return jax.shard_map(
        on_device, mesh=mesh, in_specs=in_specs, out_specs=out_specs, check_vma=False
    )
```

```python
import functools

import jax
import jax.numpy as jnp
from jax import lax
from jax.experimental import pallas as pl
from jax.experimental.pallas import tpu as pltpu
from jax.sharding import PartitionSpec as P

KVH = 8
HD = 128
WINDOW = 256


EPS = 1e-05


def rope_tables(position):
    half = HD // 2
    inverse = 500000.0 ** (-(jnp.arange(half, dtype=jnp.float32) * 2.0 / HD))
    angle = position[:, None] * inverse[None, :]
    return (jnp.cos(angle), jnp.sin(angle))


def rotate(values, cosine, sine):
    half = values.shape[-1] // 2
    first = values[..., :half]
    second = values[..., half:]
    cosine = cosine[:, None, :]
    sine = sine[:, None, :]
    return jnp.concatenate(
        [first * cosine - second * sine, second * cosine + first * sine], axis=-1
    )


SKEW = 6


def greet_peers(n):
    me = lax.axis_index("wa")
    barrier = pltpu.get_barrier_semaphore()
    for d in range(1, n):
        pl.semaphore_signal(
            barrier,
            inc=1,
            device_id={"wa": lax.rem(me + d, n)},
            device_id_type=pl.DeviceIdType.MESH,
        )
    pl.semaphore_wait(barrier, n - 1)


def send_to(src, dst, send_sem, recv_sem, peer):
    return pltpu.make_async_remote_copy(
        src_ref=src,
        dst_ref=dst,
        send_sem=send_sem,
        recv_sem=recv_sem,
        device_id={"wa": peer},
        device_id_type=pl.DeviceIdType.MESH,
    )


def peer_copies(n, x_ref, land, sems):
    me = lax.axis_index("wa")
    return [
        send_to(x_ref, land.at[d - 1], sems.at[0, d - 1], sems.at[1, d - 1], lax.rem(me + d, n))
        for d in range(1, n)
    ]


def peer_sum_kernel(n, x_ref, o_ref, land, sems):
    greet_peers(n)
    copies = peer_copies(n, x_ref, land, sems)
    for copy in copies:
        copy.start()
    for copy in copies:
        copy.wait()
    total = x_ref[...]
    for d in range(n - 1):
        total = total + land[d]
    o_ref[...] = total


def peer_sum(x, n):
    vmem = pl.BlockSpec(memory_space=pltpu.VMEM)
    return pl.pallas_call(
        functools.partial(peer_sum_kernel, n),
        out_shape=jax.ShapeDtypeStruct(x.shape, x.dtype),
        in_specs=[vmem],
        out_specs=vmem,
        scratch_shapes=[
            pltpu.VMEM((n - 1,) + x.shape, x.dtype),
            pltpu.SemaphoreType.DMA((2, n - 1)),
        ],
        compiler_params=pltpu.CompilerParams(
            collective_id=2, has_side_effects=True, vmem_limit_bytes=4 << 20
        ),
    )(x)


def reduce_kernel(
    n, nc, half, window, q_ref, kv_ref, sq_ref, qo, kvo, sqo,
    rq, rkv, lq, lkv, lsq, rqs, rks, lqs, lks, sqs,
):
    me = lax.axis_index("wa")
    last = n - 1
    right = jnp.minimum(me + 1, last)
    left = jnp.maximum(me - 1, 0)
    cq = half // nc
    cw = (half + window) // nc
    greet_peers(n)
    small = peer_copies(n, sq_ref, lsq, sqs)
    for copy in small:
        copy.start()
    kvo[pl.ds(0, window), :] = jnp.zeros((window, kvo.shape[1]), kvo.dtype)

    def rows(base, j, size):
        return pl.ds(pl.multiple_of(base + j * size, 8), size)

    def right_copy(j, first_hop):
        own, wide = rows(0, j, cq), rows(0, j, cw)
        if first_hop:
            src, src_kv = q_ref.at[rows(half, j, cq)], kv_ref.at[rows(half - window, j, cw)]
        else:
            src, src_kv = rq.at[own], rkv.at[wide]
        return (
            send_to(src, rq.at[own], rqs.at[0, j], rqs.at[1, j], right),
            send_to(src_kv, rkv.at[wide], rks.at[0, j], rks.at[1, j], right),
        )

    def left_copy(j, first_hop):
        own = rows(0, j, cq)
        src, src_kv = (q_ref, kv_ref) if first_hop else (lq, lkv)
        return (
            send_to(src.at[own], lq.at[own], lqs.at[0, j], lqs.at[1, j], left),
            send_to(src_kv.at[own], lkv.at[own], lks.at[0, j], lks.at[1, j], left),
        )

    @pl.loop(0, nc + SKEW * last)
    def _(s):
        j = s - SKEW * me
        i = s - SKEW * (last - me)
        right_on = (j >= 0) & (j < nc)
        left_on = (i >= 0) & (i < nc)

        @pl.when(right_on & (me > 0))
        def _():
            for copy in right_copy(j, False):
                copy.wait_recv()
            own, wide = rows(0, j, cq), rows(0, j, cw)
            rq[own, :] = rq[own, :] + q_ref[rows(half, j, cq), :]
            rkv[wide, :] = rkv[wide, :] + kv_ref[rows(half - window, j, cw), :]

        @pl.when(left_on & (me < last))
        def _():
            for copy in left_copy(i, False):
                copy.wait_recv()
            own = rows(0, i, cq)
            lq[own, :] = lq[own, :] + q_ref[own, :]
            lkv[own, :] = lkv[own, :] + kv_ref[own, :]

        @pl.when(right_on & (me == 0))
        def _():
            for copy in right_copy(j, True):
                copy.start()

        @pl.when(left_on & (me == last))
        def _():
            for copy in left_copy(i, True):
                copy.start()

        @pl.when(right_on & (me > 0) & (me < last))
        def _():
            for copy in right_copy(j, False):
                copy.start()

        @pl.when(left_on & (me > 0) & (me < last))
        def _():
            for copy in left_copy(i, False):
                copy.start()

        @pl.when(right_on & (me == last))
        def _():
            own, wide = rows(0, j, cq), rows(0, j, cw)
            qo[own, :] = rq[own, :]
            kvo[wide, :] = rkv[wide, :]

        @pl.when(left_on & (me < last))
        def _():
            own = rows(0, i, cq)
            qo[own, :] = lq[own, :]
            kvo[rows(window, i, cq), :] = lkv[own, :]

    @pl.loop(0, nc)
    def _(j):
        @pl.when(me < last)
        def _():
            for copy in right_copy(j, False):
                copy.wait_send()

        @pl.when(me > 0)
        def _():
            for copy in left_copy(j, False):
                copy.wait_send()

    for copy in small:
        copy.wait()
    total = sq_ref[...]
    for d in range(n - 1):
        total = total + lsq[d]
    sqo[...] = total


def reduce_to_ends(q_part, kv_part, row_sq, n, window):
    rows, cols = q_part.shape
    kv_cols = kv_part.shape[1]
    half = rows // 2
    nc = half // 16
    vmem = pl.BlockSpec(memory_space=pltpu.VMEM)
    f32 = jnp.float32
    pair = pltpu.SemaphoreType.DMA((2, nc))
    return pl.pallas_call(
        functools.partial(reduce_kernel, n, nc, half, window),
        out_shape=(
            jax.ShapeDtypeStruct((half, cols), f32),
            jax.ShapeDtypeStruct((half + window, kv_cols), f32),
            jax.ShapeDtypeStruct(row_sq.shape, f32),
        ),
        in_specs=[vmem] * 3,
        out_specs=(vmem,) * 3,
        scratch_shapes=[
            pltpu.VMEM((half, cols), f32),
            pltpu.VMEM((half + window, kv_cols), f32),
            pltpu.VMEM((half, cols), f32),
            pltpu.VMEM((half, kv_cols), f32),
            pltpu.VMEM((n - 1,) + row_sq.shape, f32),
            pair,
            pair,
            pair,
            pair,
            pltpu.SemaphoreType.DMA((2, n - 1)),
        ],
        compiler_params=pltpu.CompilerParams(
            collective_id=0, has_side_effects=True, vmem_limit_bytes=40 << 20
        ),
    )(q_part, kv_part, row_sq)


def spread_kernel(n, nc, half, x_ref, o_ref, rs, ls):
    me = lax.axis_index("wa")
    last = n - 1
    right = jnp.minimum(me + 1, last)
    left = jnp.maximum(me - 1, 0)
    size = half // nc
    greet_peers(n)

    def rows(base, j):
        return pl.ds(pl.multiple_of(base + j * size, 16), size)

    def right_copy(j, first_hop):
        at = rows(0, j)
        src = x_ref if first_hop else o_ref
        return send_to(src.at[at], o_ref.at[at], rs.at[0, j], rs.at[1, j], right)

    def left_copy(j, first_hop):
        at = rows(half, j)
        src = x_ref.at[rows(0, j)] if first_hop else o_ref.at[at]
        return send_to(src, o_ref.at[at], ls.at[0, j], ls.at[1, j], left)

    @pl.loop(0, nc + SKEW * last)
    def _(s):
        j = s - SKEW * me
        i = s - SKEW * (last - me)
        right_on = (j >= 0) & (j < nc)
        left_on = (i >= 0) & (i < nc)

        @pl.when(right_on & (me == 0))
        def _():
            right_copy(j, True).start()
            o_ref[rows(0, j), :] = x_ref[rows(0, j), :]

        @pl.when(left_on & (me == last))
        def _():
            left_copy(i, True).start()
            o_ref[rows(half, i), :] = x_ref[rows(0, i), :]

        @pl.when(right_on & (me > 0))
        def _():
            right_copy(j, False).wait_recv()

        @pl.when(right_on & (me > 0) & (me < last))
        def _():
            right_copy(j, False).start()

        @pl.when(left_on & (me < last))
        def _():
            left_copy(i, False).wait_recv()

        @pl.when(left_on & (me > 0) & (me < last))
        def _():
            left_copy(i, False).start()

    @pl.loop(0, nc)
    def _(j):
        @pl.when(me < last)
        def _():
            right_copy(j, False).wait_send()

        @pl.when(me > 0)
        def _():
            left_copy(j, False).wait_send()


def spread_from_ends(x, n):
    half, cols = x.shape
    nc = half // 16
    vmem = pl.BlockSpec(memory_space=pltpu.VMEM)
    pair = pltpu.SemaphoreType.DMA((2, nc))
    return pl.pallas_call(
        functools.partial(spread_kernel, n, nc, half),
        out_shape=jax.ShapeDtypeStruct((2 * half, cols), x.dtype),
        in_specs=[vmem],
        out_specs=vmem,
        scratch_shapes=[pair, pair],
        compiler_params=pltpu.CompilerParams(
            collective_id=1, has_side_effects=True, vmem_limit_bytes=16 << 20
        ),
    )(x)


def attend(queries, key_head, value_head, segment_ids, first):
    q_rows = queries.shape[0]
    size = min(WINDOW, q_rows)
    segment_pad = jnp.pad(segment_ids, (WINDOW, 0), constant_values=-1)
    outs = []
    for at in range(0, q_rows, size):
        start = first + at
        query = queries[at : at + size]
        key = key_head[at : at + size + WINDOW]
        value = value_head[at : at + size + WINDOW]
        k_segment = lax.dynamic_slice_in_dim(segment_pad, start, size + WINDOW, 0)
        q_segment = lax.dynamic_slice_in_dim(segment_ids, start, size, 0)
        k_at = jnp.arange(size + WINDOW, dtype=jnp.int32) - WINDOW
        q_at = jnp.arange(size, dtype=jnp.int32)
        allowed = (q_segment[:, None] == k_segment[None, :]) & (k_at[None, :] <= q_at[:, None])
        allowed = allowed & (k_at + start >= 0)[None, :]
        scores = jnp.einsum(
            "thd,sd->hts", query, key, preferred_element_type=jnp.float32
        ) * HD ** (-0.5)
        scores = jnp.where(allowed[None], scores, -1e30)
        peak = jnp.max(scores, axis=-1, keepdims=True)
        expo = jnp.where(allowed[None], jnp.exp(scores - peak), 0.0)
        weights = (expo / jnp.sum(expo, axis=-1, keepdims=True)).astype(jnp.bfloat16)
        out = jnp.einsum("hts,sd->thd", weights, value, preferred_element_type=jnp.float32)
        outs.append(out.astype(jnp.bfloat16))
    return jnp.concatenate(outs, axis=0)


def on_device(tokens, gain_attn, w_query, w_key, w_value, w_out, gain_ffn, segment_ids):
    rows_dev, width_dev = tokens.shape
    n_wa = lax.axis_size("wa")
    n_ha = lax.axis_size("ha")
    total = rows_dev * n_ha
    width = width_dev * n_wa
    head_cols = w_query.shape[1]
    heads_dev = head_cols // HD
    token_f = tokens.astype(jnp.float32)
    gain_one = gain_attn.astype(jnp.float32)
    kv_head = lax.axis_index("ha") // (n_ha // KVH)
    kv_weights = jnp.concatenate(
        [
            lax.dynamic_slice_in_dim(w_key, kv_head * HD, HD, 1),
            lax.dynamic_slice_in_dim(w_value, kv_head * HD, HD, 1),
        ],
        axis=1,
    )
    gathered = lax.all_gather(tokens, "ha", axis=0, tiled=True)
    gathered_f = gathered.astype(jnp.float32)
    row_sq = jnp.sum(gathered_f * gathered_f, axis=1)
    scaled = (gathered_f * gain_one).astype(jnp.bfloat16)
    kv_part = jnp.dot(scaled, kv_weights, preferred_element_type=jnp.float32)
    q_part = jnp.dot(scaled, w_query, preferred_element_type=jnp.float32)
    lanes = min(total, 128)
    query_f, kv_sum, sq_sum = reduce_to_ends(
        q_part, kv_part, row_sq.reshape(total // lanes, lanes), n_wa, WINDOW
    )
    row_scale = lax.rsqrt(sq_sum.reshape(total) / width + EPS)
    q_rows = total // 2
    first = jnp.where(lax.axis_index("wa") == n_wa - 1, q_rows, 0)
    kv_rows = q_rows + WINDOW

    def around(table):
        padded = jnp.pad(table, ((WINDOW, 0),) + ((0, 0),) * (table.ndim - 1))
        return lax.dynamic_slice_in_dim(padded, first, kv_rows, 0)

    index_all = jnp.arange(total, dtype=jnp.int32)
    fresh = jnp.concatenate([jnp.ones((1,), dtype=bool), segment_ids[1:] != segment_ids[:-1]])
    start_all = lax.cummax(jnp.where(fresh, index_all, jnp.zeros_like(index_all)), axis=0)
    cosine, sine = rope_tables((index_all - start_all).astype(jnp.float32))
    scale = around(row_scale)
    cosine, sine = around(cosine), around(sine)
    key_plain = (kv_sum[:, :HD] * scale[:, None]).astype(jnp.bfloat16)
    key_plain = lax.optimization_barrier(key_plain)
    value_head = (kv_sum[:, HD:] * scale[:, None]).astype(jnp.bfloat16)
    key_head = rotate(key_plain.astype(jnp.float32).reshape(kv_rows, 1, HD), cosine, sine)
    key_head = key_head.reshape(kv_rows, HD).astype(jnp.bfloat16)
    q_scale, q_cos, q_sin = scale[WINDOW:], cosine[WINDOW:], sine[WINDOW:]
    queries = rotate(
        (query_f * q_scale[:, None]).reshape(q_rows, heads_dev, HD), q_cos, q_sin
    ).astype(jnp.bfloat16)
    head_out = attend(queries, key_head, value_head, segment_ids, first)
    head_out = head_out.reshape(q_rows, head_cols)
    head_all = spread_from_ends(head_out, n_wa)
    block = head_all
    attended = lax.psum_scatter(
        jnp.dot(block, w_out, preferred_element_type=jnp.float32).astype(jnp.bfloat16),
        "ha",
        scatter_dimension=0,
        tiled=True,
    )
    residual_out = (token_f + attended.astype(jnp.float32)).astype(jnp.bfloat16)
    residual_f = residual_out.astype(jnp.float32)
    own_two = jnp.sum(residual_f * residual_f, axis=1)
    own_two = jnp.pad(own_two, (0, -rows_dev % 128)).reshape(-1, 128)
    square_two = peer_sum(own_two, n_wa).reshape(-1)[:rows_dev]
    scale_two = lax.rsqrt(square_two / width + EPS)
    ffn_input = (residual_f * scale_two[:, None] * gain_ffn.astype(jnp.float32)).astype(
        jnp.bfloat16
    )
    return (residual_out, ffn_input)


def solution(mesh):
    in_specs = (
        P("ha", "wa"),
        P("wa"),
        P("wa", "ha"),
        P("wa", None),
        P("wa", None),
        P("ha", "wa"),
        P("wa"),
        P(),
    )
    out_specs = (P("ha", "wa"), P("ha", "wa"))
    return jax.shard_map(
        on_device, mesh=mesh, in_specs=in_specs, out_specs=out_specs, check_vma=False
    )
```
